32 devices in a mesh: outer: 4 (over z), inner: 2 (over x), head: 4 (over y, core).
Axes of the slice: x: 2, y: 2, z: 4, core: 2. Of those that a mesh axis runs over, the one named last changes fastest.
Arguments:
- queries: bfloat16 [1024, 4096], P(('outer', 'inner'), 'head'), may hold values from -6 to 6
- keys: bfloat16 [1024, 512], P(('outer', 'inner'), 'head'), may hold values from -6 to 6
- values: bfloat16 [1024, 512], P(('outer', 'inner'), 'head'), may hold values from -6 to 6
- doc_start: int32 [1024], P(('outer', 'inner')), may hold values from 0 to 1023, as said below
- w_out: bfloat16 [4096, 4096], P('head'), may hold values from -0.09375 to 0.09375
Outputs:
- block_out: bfloat16 [1024, 4096], P(('outer', 'inner'))
The draws below stay inside these ranges and needn't reach their ends.
Inputs may be any that keep to these rules, and one draw needn't show every extreme that they name: doc_start[t] is the first position of the document that holds token t: it never falls, doc_start[t] <= t, it equals t where a document begins, and documents hold 1 to 512 tokens, at least one exactly 512; the last token begins a document of its own.
All inputs are finite; a program needn't handle non-finite values.
Results may differ from the reference program's by a relative error of at most 0.01.
Values may be sent and summed in bfloat16 or wider, within the bound.
A program may use at most 64 MiB of HBM per device.

```python
import jax
import jax.numpy as jnp
from jax import lax

QUERY_HEADS = 32
KEY_VALUE_HEADS = 4
HEAD_SIZE = 128
DOUT = 4096
TOK_DEV = 128
PACKED_TOKENS = 1024
DOCUMENT_LIMIT = 512
N_INNER = 2
N_HEAD = 4


def random_rows(key, width):
    first_key = jax.random.fold_in(key, 0)
    return jnp.clip(jax.random.normal(first_key, (PACKED_TOKENS, width), jnp.float32), -6.0, 6.0)


def draw_queries(key, part):
    row_list = random_rows(jax.random.fold_in(key, 31), QUERY_HEADS * HEAD_SIZE)
    return row_list.astype(jnp.bfloat16)


def draw_keys(key, part):
    row_list = random_rows(jax.random.fold_in(key, 37), KEY_VALUE_HEADS * HEAD_SIZE)
    return row_list.astype(jnp.bfloat16)


def draw_doc_start(key, part):
    first_key, second_key = jax.random.split(jax.random.fold_in(key, 23))
    position = jnp.arange(PACKED_TOKENS, dtype=jnp.int32)
    marked = jax.random.randint(first_key, (PACKED_TOKENS,), 0, DOCUMENT_LIMIT) < 4
    anchor = jax.random.randint(second_key, (), 0, PACKED_TOKENS - DOCUMENT_LIMIT)
    inside = (position > anchor) & (position < anchor + DOCUMENT_LIMIT)
    marked = marked & jnp.logical_not(inside) | (position == anchor) | (position == anchor + DOCUMENT_LIMIT) | (position == 0) | (position == PACKED_TOKENS - 1)

    def walk(latest, item):
        where_at, flagged = item
        begin = jnp.where(flagged | (where_at - latest >= DOCUMENT_LIMIT), where_at, latest)
        return (begin, begin)
    unused, starts = lax.scan(walk, jnp.int32(0), (position, marked))
    return starts.astype(jnp.int32)


def steps_of(own_key, shape, shards, smallest, high):
    loudness = 1.0
    for dim, parts in shards:
        steps = jax.random.uniform(jax.random.fold_in(jax.random.fold_in(own_key, 6), dim), (parts,), jnp.float32, smallest / len(shards), high / len(shards))
        loudness = loudness * jnp.repeat(jnp.exp(steps), shape[dim] // parts).reshape((-1,) + (1,) * (len(shape) - 1 - dim))
    return loudness


def normal_values(rng, extent, scale, most, cuts=(), kind=jnp.bfloat16):
    level = steps_of(rng, extent, cuts, -0.22, 0.18) if cuts else 1.0
    values = jax.random.normal(rng, extent, jnp.float32) * scale * level
    return jnp.minimum(jnp.maximum(values, -most), most).astype(kind)


def setup_inputs(seed: int = 0) -> dict:
    arg_keys = jax.random.split(jax.random.key(seed), 6)
    queries = draw_queries(jax.random.fold_in(arg_keys[5], 71), 0)
    keys = draw_keys(jax.random.fold_in(arg_keys[5], 71), 0)
    values = normal_values(arg_keys[2], (PACKED_TOKENS, KEY_VALUE_HEADS * HEAD_SIZE), 1.0, 6.0, ((0, 8), (1, 4)))
    doc_start = draw_doc_start(jax.random.fold_in(arg_keys[5], 71), 0)
    w_out = normal_values(arg_keys[4], (QUERY_HEADS * HEAD_SIZE, DOUT), (QUERY_HEADS * HEAD_SIZE) ** -0.5, 0.09375, ((0, 4),))
    return dict(queries=queries, keys=keys, values=values, doc_start=doc_start, w_out=w_out)


masked_fill = -1e30


def reference(queries, keys, values, doc_start, w_out):
    head_portion = QUERY_HEADS // KEY_VALUE_HEADS
    tile_block = min(512, TOK_DEV * N_INNER)
    count = PACKED_TOKENS // tile_block
    scale = HEAD_SIZE ** -0.5
    padded_keys = jnp.concatenate([jnp.zeros((DOCUMENT_LIMIT, KEY_VALUE_HEADS * HEAD_SIZE), jnp.bfloat16), keys], 0)
    padded_values = jnp.concatenate([jnp.zeros((DOCUMENT_LIMIT, KEY_VALUE_HEADS * HEAD_SIZE), jnp.bfloat16), values], 0)
    document_extent = DOCUMENT_LIMIT + tile_block

    def one_block(index):
        first_row_index = (index * tile_block).astype(jnp.int32)
        query_matrix = lax.dynamic_slice_in_dim(queries, first_row_index, tile_block, 0).astype(jnp.float32).reshape(tile_block, KEY_VALUE_HEADS, head_portion, HEAD_SIZE)
        key_matrix = lax.dynamic_slice_in_dim(padded_keys, first_row_index, document_extent, 0).astype(jnp.float32).reshape(document_extent, KEY_VALUE_HEADS, HEAD_SIZE)
        value_matrix = lax.dynamic_slice_in_dim(padded_values, first_row_index, document_extent, 0).astype(jnp.float32).reshape(document_extent, KEY_VALUE_HEADS, HEAD_SIZE)
        starts = lax.dynamic_slice_in_dim(doc_start, first_row_index, tile_block, 0)
        query_pos = first_row_index + jnp.arange(tile_block, dtype=jnp.int32)
        key_pos = first_row_index - DOCUMENT_LIMIT + jnp.arange(document_extent, dtype=jnp.int32)
        visible = (key_pos[None, :] >= starts[:, None]) & (key_pos[None, :] <= query_pos[:, None])
        scores = jnp.einsum("tkgd,skd->kgts", query_matrix, key_matrix) * scale
        masked = jnp.where(visible, scores, masked_fill)
        peak = jnp.max(masked, axis=-1)
        weights = jnp.where(visible, jnp.exp(masked - peak[..., None]), 0.0)
        total = jnp.sum(weights, axis=-1)
        rounded = lax.optimization_barrier(weights.astype(jnp.bfloat16)).astype(jnp.float32)
        mixed = jnp.einsum("kgts,skd->kgtd", rounded, value_matrix) / total[..., None]
        return mixed.transpose(2, 0, 1, 3).reshape(tile_block, QUERY_HEADS * HEAD_SIZE).astype(jnp.bfloat16)

    attended = lax.map(one_block, jnp.arange(count, dtype=jnp.int32)).reshape(PACKED_TOKENS, QUERY_HEADS * HEAD_SIZE)
    row_list = QUERY_HEADS // N_HEAD * HEAD_SIZE
    result = jnp.zeros((PACKED_TOKENS, DOUT), jnp.float32)
    for group in range(N_HEAD):
        piece = jnp.dot(attended[:, group * row_list:(group + 1) * row_list], w_out[group * row_list:(group + 1) * row_list], preferred_element_type=jnp.float32)
        piece = lax.optimization_barrier(piece.astype(jnp.bfloat16))
        result = result + piece.astype(jnp.float32)
    return result.astype(jnp.bfloat16)
```

```python
import functools
import math

import jax
import jax.numpy as jnp
from jax import lax
from jax.experimental import pallas as pl
from jax.experimental.pallas import tpu as pltpu
from jax.sharding import PartitionSpec as P

HEAD_SIZE = 128
CHUNK = 256
masked_fill = -1e30
MESH = pl.DeviceIdType.MESH


def kernel(
    n_outer, n_inner, reach,
    q_hbm, k_hbm, v_hbm, ds_hbm, w_hbm, out_ref,
    q_v, ds_v, kbuf, vbuf, wbuf, m_ref, l_ref, acc, att,
    p_other, p_own, p_recv, a_own, a_recv, y_recv, y_pair,
    local_sem, w_sem, kv_recv, z_send, x_send,
    pair_s, pair_r, ypush_s, ypush_r, asum_s, asum_r, relay_s, relay_r,
):
    tok = q_hbm.shape[0]
    heads = q_hbm.shape[1] // HEAD_SIZE
    half = w_hbm.shape[1] // 2
    n_chunk = half // CHUNK
    group_len = tok * n_inner
    o = lax.axis_index("outer")
    i = lax.axis_index("inner")
    h = lax.axis_index("head")
    side = lax.rem(h, 2)
    pair_h = h + 1 - 2 * side
    y_h = lax.rem(h + 2, 4)
    pair_dev = (o, i, pair_h)
    y_dev = (o, i, y_h)

    loads = [
        pltpu.make_async_copy(q_hbm, q_v, local_sem.at[0]),
        pltpu.make_async_copy(ds_hbm, ds_v, local_sem.at[1]),
        pltpu.make_async_copy(k_hbm, kbuf.at[0, i], local_sem.at[2]),
        pltpu.make_async_copy(v_hbm, vbuf.at[0, i], local_sem.at[3]),
    ]
    for load in loads:
        load.start()
    own_col = side * half
    other_col = (1 - side) * half
    w_loads = []
    for c in range(n_chunk):
        for which, base in ((0, other_col), (1, own_col)):
            col = pl.multiple_of(base + c * CHUNK, CHUNK)
            w_loads.append(
                pltpu.make_async_copy(
                    w_hbm.at[:, pl.ds(col, CHUNK)], wbuf.at[2 * c + which], w_sem.at[2 * c + which]
                )
            )

    def used(d, j):
        ok = o >= d
        if d == 0:
            ok = ok & (j <= i)
        if d == reach:
            ok = ok & (j >= i)
        return ok

    def sends_x(d, j):
        ok = o >= d
        if d == 0:
            ok = ok & (j > i)
        if d == reach:
            ok = ok & (j < i)
        return ok

    zeros = jnp.zeros((tok, HEAD_SIZE), jnp.bfloat16)
    for d in range(reach + 1):
        for r in range(n_inner):
            if d == 0 and r == 0:
                continue
            j = lax.rem(i + r, n_inner)

            @pl.when(jnp.logical_not(used(d, j)))
            def _(d=d, j=j):
                kbuf[d, j] = zeros
                vbuf[d, j] = zeros

    barrier = pltpu.get_barrier_semaphore()
    for peer in (pair_dev, y_dev):
        pl.semaphore_signal(barrier, inc=1, device_id=peer, device_id_type=MESH)
    for r in range(1, n_inner):
        pl.semaphore_signal(
            barrier, inc=1, device_id=(o, lax.rem(i + r, n_inner), h), device_id_type=MESH
        )

    @pl.when(o > 0)
    def _():
        pl.semaphore_signal(barrier, inc=1, device_id=(o - 1, i, h), device_id_type=MESH)

    @pl.when(o < n_outer - 1)
    def _():
        pl.semaphore_signal(barrier, inc=1, device_id=(o + 1, i, h), device_id_type=MESH)

    behind = jnp.where(o > 0, 1, 0)
    ahead = jnp.where(o < n_outer - 1, 1, 0)
    pl.semaphore_wait(barrier, 1 + n_inner + behind + ahead)

    bufs = (kbuf, vbuf)
    hbms = (k_hbm, v_hbm)

    def z_copy(t, d):
        src = hbms[t] if d == 0 else bufs[t].at[d, i]
        return pltpu.make_async_remote_copy(
            src_ref=src, dst_ref=bufs[t].at[d + 1, i],
            send_sem=z_send.at[t, d], recv_sem=kv_recv.at[t, d + 1, i],
            device_id=(o + 1, i, h), device_id_type=MESH,
        )

    def x_copy(t, d, r):
        src = hbms[t] if d == 0 else bufs[t].at[d, i]
        return pltpu.make_async_remote_copy(
            src_ref=src, dst_ref=bufs[t].at[d, i],
            send_sem=x_send.at[t, d, r], recv_sem=kv_recv.at[t, d, i],
            device_id=(o, lax.rem(i + r, n_inner), h), device_id_type=MESH,
        )

    def arrival(t, d, j):
        return pltpu.make_async_remote_copy(
            src_ref=bufs[t].at[d, j], dst_ref=bufs[t].at[d, j],
            send_sem=z_send.at[t, 0], recv_sem=kv_recv.at[t, d, j],
            device_id=(o, lax.rem(i + 1, n_inner), h), device_id_type=MESH,
        )

    def z_ok(d):
        return (o >= d) & (o < n_outer - 1)

    def forward(t, d):
        if d < reach:
            @pl.when(z_ok(d))
            def _():
                z_copy(t, d).start()
        for r in range(1, n_inner):
            @pl.when(sends_x(d, lax.rem(i + r, n_inner)))
            def _():
                x_copy(t, d, r).start()

    for t in range(2):
        forward(t, 0)
    for w_load in w_loads:
        w_load.start()

    coef = HEAD_SIZE ** (-0.5) * math.log2(math.e)
    start_pos = (o * n_inner + i) * tok

    def visit(d):
        for r in range(1, n_inner):
            j = lax.rem(i + r, n_inner)

            @pl.when(used(d, j))
            def _():
                for t in range(2):
                    arrival(t, d, j).wait_recv()
        k = kbuf[d].reshape(group_len, HEAD_SIZE)
        v_t = vbuf[d].reshape(group_len, HEAD_SIZE).T
        key_pos = (o - d) * group_len + lax.broadcasted_iota(jnp.int32, (group_len, tok), 0)
        query_pos = start_pos + lax.broadcasted_iota(jnp.int32, (group_len, tok), 1)
        starts = ds_v[...].reshape(1, tok)
        visible = (key_pos >= starts) & (key_pos <= query_pos)
        for g in range(heads):
            q = q_v[:, g * HEAD_SIZE:(g + 1) * HEAD_SIZE]
            s = lax.dot_general(k, q, (((1,), (1,)), ((), ())), preferred_element_type=jnp.float32)
            s = jnp.where(visible, s, masked_fill)
            top = jnp.max(s, axis=0, keepdims=True)
            if d == 0:
                peak = top
            else:
                peak = jnp.maximum(m_ref[g:g + 1], top)
                fade = jnp.exp2((m_ref[g:g + 1] - peak) * coef)
            p = jnp.exp2((s - peak) * coef)
            total = jnp.sum(p, axis=0, keepdims=True)
            mixed = jnp.dot(v_t, p.astype(jnp.bfloat16), preferred_element_type=jnp.float32)
            if d > 0:
                total = total + l_ref[g:g + 1] * fade
                mixed = mixed + acc[g] * fade
            if d < reach:
                m_ref[g:g + 1] = peak
                l_ref[g:g + 1] = total
                acc[g] = mixed
            else:
                att[:, g * HEAD_SIZE:(g + 1) * HEAD_SIZE] = (
                    (mixed * (1.0 / total)).T.astype(jnp.bfloat16)
                )

    for load in loads:
        load.wait()
    for d in range(1, reach + 1):
        for t in range(2):
            @pl.when(o >= d)
            def _():
                arrival(t, d, i).wait_recv()
            forward(t, d)
        visit(d - 1)
    visit(reach)

    def to_pair(c):
        return pltpu.make_async_remote_copy(
            src_ref=p_other.at[c], dst_ref=p_recv.at[c],
            send_sem=pair_s.at[c], recv_sem=pair_r.at[c],
            device_id=pair_dev, device_id_type=MESH,
        )

    def to_y(c):
        return pltpu.make_async_remote_copy(
            src_ref=a_own.at[c], dst_ref=y_recv.at[c],
            send_sem=ypush_s.at[c], recv_sem=ypush_r.at[c],
            device_id=y_dev, device_id_type=MESH,
        )

    def sum_to_pair(c):
        return pltpu.make_async_remote_copy(
            src_ref=a_own.at[c], dst_ref=a_recv.at[c],
            send_sem=asum_s.at[c], recv_sem=asum_r.at[c],
            device_id=pair_dev, device_id_type=MESH,
        )

    def relay(c):
        return pltpu.make_async_remote_copy(
            src_ref=y_recv.at[c], dst_ref=y_pair.at[c],
            send_sem=relay_s.at[c], recv_sem=relay_r.at[c],
            device_id=pair_dev, device_id_type=MESH,
        )

    def product(slot):
        w_loads[slot].wait()
        return jnp.dot(att[...], wbuf[slot], preferred_element_type=jnp.float32).astype(jnp.bfloat16)

    def join(c):
        to_pair(c).wait_recv()
        a_own[c] = (
            p_own[c].astype(jnp.float32) + p_recv[c].astype(jnp.float32)
        ).astype(jnp.bfloat16)
        to_y(c).start()
        sum_to_pair(c).start()

    for c in range(n_chunk):
        p_other[c] = product(2 * c)
        to_pair(c).start()
        p_own[c] = product(2 * c + 1)
        if c >= 1:
            join(c - 1)
    join(n_chunk - 1)

    def finish(c):
        sum_to_pair(c).wait_recv()
        relay(c).wait_recv()
        col = pl.multiple_of(other_col + c * CHUNK, CHUNK)
        out_ref[:, pl.ds(col, CHUNK)] = (
            a_recv[c].astype(jnp.float32) + y_pair[c].astype(jnp.float32)
        ).astype(jnp.bfloat16)

    for c in range(n_chunk):
        to_y(c).wait_recv()
        relay(c).start()
        col = pl.multiple_of(own_col + c * CHUNK, CHUNK)
        out_ref[:, pl.ds(col, CHUNK)] = (
            a_own[c].astype(jnp.float32) + y_recv[c].astype(jnp.float32)
        ).astype(jnp.bfloat16)
        if c >= 1:
            finish(c - 1)
    finish(n_chunk - 1)

    for t in range(2):
        for d in range(reach + 1):
            if d < reach:
                @pl.when(z_ok(d))
                def _():
                    z_copy(t, d).wait_send()
            for r in range(1, n_inner):
                @pl.when(sends_x(d, lax.rem(i + r, n_inner)))
                def _():
                    x_copy(t, d, r).wait_send()
    for c in range(n_chunk):
        to_pair(c).wait_send()
        to_y(c).wait_send()
        sum_to_pair(c).wait_send()
        relay(c).wait_send()


def shards(n_outer, n_inner, queries, keys, values, doc_start, w_out):
    tok = queries.shape[0]
    heads = queries.shape[1] // HEAD_SIZE
    dout = w_out.shape[1]
    reach = min(8, n_outer // 2)
    n_chunk = dout // 2 // CHUNK
    bf16, f32 = jnp.bfloat16, jnp.float32
    dma = pltpu.SemaphoreType.DMA
    slots = (reach + 1, n_inner, tok, HEAD_SIZE)
    piece = pltpu.VMEM((n_chunk, tok, CHUNK), bf16)
    any_spec = pl.BlockSpec(memory_space=pltpu.HBM)
    return pl.pallas_call(
        functools.partial(kernel, n_outer, n_inner, reach),
        out_shape=jax.ShapeDtypeStruct((tok, dout), bf16),
        in_specs=[any_spec] * 5,
        out_specs=pl.BlockSpec(memory_space=pltpu.VMEM),
        scratch_shapes=[
            pltpu.VMEM(queries.shape, bf16),
            pltpu.VMEM((tok,), jnp.int32),
            pltpu.VMEM(slots, bf16),
            pltpu.VMEM(slots, bf16),
            pltpu.VMEM((2 * n_chunk, w_out.shape[0], CHUNK), bf16),
            pltpu.VMEM((heads, tok), f32),
            pltpu.VMEM((heads, tok), f32),
            pltpu.VMEM((heads, HEAD_SIZE, tok), f32),
            pltpu.VMEM((tok, heads * HEAD_SIZE), bf16),
            piece, piece, piece, piece, piece, piece, piece,
            dma((4,)),
            dma((2 * n_chunk,)),
            dma((2, reach + 1, n_inner)),
            dma((2, reach)),
            dma((2, reach + 1, n_inner)),
        ] + [dma((n_chunk,))] * 8,
        compiler_params=pltpu.CompilerParams(
            collective_id=0, has_side_effects=True, vmem_limit_bytes=67043328
        ),
    )(queries, keys, values, doc_start, w_out)


def solution(mesh):
    placed = (
        P(("outer", "inner"), "head"),
        P(("outer", "inner"), "head"),
        P(("outer", "inner"), "head"),
        P(("outer", "inner")),
        P("head", None),
    )
    body = functools.partial(shards, mesh.shape["outer"], mesh.shape["inner"])
    return jax.shard_map(
        body, mesh=mesh, in_specs=placed, out_specs=P(("outer", "inner"), None), check_vma=False
    )
```

```python
import functools
import math

import jax
import jax.numpy as jnp
from jax import lax
from jax.experimental import pallas as pl
from jax.experimental.pallas import tpu as pltpu
from jax.sharding import PartitionSpec as P

HEAD_SIZE = 128
CHUNK = 256
masked_fill = -1e30
MESH = pl.DeviceIdType.MESH


def kernel(
    n_outer, n_inner, reach,
    q_hbm, k_hbm, v_hbm, ds_hbm, w_hbm, out_ref,
    q_v, ds_v, kbuf, vbuf, wbuf, m_ref, l_ref, acc, att,
    p_other, p_own, p_recv, a_own, a_recv, y_recv, y_pair,
    local_sem, w_sem, kv_recv, z_send, x_send,
    pair_s, pair_r, ypush_s, ypush_r, asum_s, asum_r, relay_s, relay_r,
):
    tok = q_hbm.shape[0]
    heads = q_hbm.shape[1] // HEAD_SIZE
    half = w_hbm.shape[1] // 2
    n_chunk = half // CHUNK
    group_len = tok * n_inner
    o = lax.axis_index("outer")
    i = lax.axis_index("inner")
    h = lax.axis_index("head")
    side = lax.rem(h, 2)
    pair_h = h + 1 - 2 * side
    y_h = lax.rem(h + 2, 4)
    pair_dev = (o, i, pair_h)
    y_dev = (o, i, y_h)

    loads = [
        pltpu.make_async_copy(q_hbm, q_v, local_sem.at[0]),
        pltpu.make_async_copy(ds_hbm, ds_v, local_sem.at[1]),
        pltpu.make_async_copy(k_hbm, kbuf.at[0, i], local_sem.at[2]),
        pltpu.make_async_copy(v_hbm, vbuf.at[0, i], local_sem.at[3]),
    ]
    for load in loads:
        load.start()
    own_col = side * half
    other_col = (1 - side) * half
    w_loads = []
    for c in range(n_chunk):
        for which, base in ((0, other_col), (1, own_col)):
            col = pl.multiple_of(base + c * CHUNK, CHUNK)
            w_loads.append(
                pltpu.make_async_copy(
                    w_hbm.at[:, pl.ds(col, CHUNK)], wbuf.at[2 * c + which], w_sem.at[2 * c + which]
                )
            )

    def used(d, j):
        ok = o >= d
        if d == 0:
            ok = ok & (j <= i)
        if d == reach:
            ok = ok & (j >= i)
        return ok

    def sends_x(d, j):
        ok = o >= d
        if d == 0:
            ok = ok & (j > i)
        if d == reach:
            ok = ok & (j < i)
        return ok

    zeros = jnp.zeros((tok, HEAD_SIZE), jnp.bfloat16)
    for d in range(reach + 1):
        for r in range(n_inner):
            if d == 0 and r == 0:
                continue
            j = lax.rem(i + r, n_inner)

            @pl.when(jnp.logical_not(used(d, j)))
            def _(d=d, j=j):
                kbuf[d, j] = zeros
                vbuf[d, j] = zeros

    barrier = pltpu.get_barrier_semaphore()
    for peer in (pair_dev, y_dev):
        pl.semaphore_signal(barrier, inc=1, device_id=peer, device_id_type=MESH)
    for r in range(1, n_inner):
        pl.semaphore_signal(
            barrier, inc=1, device_id=(o, lax.rem(i + r, n_inner), h), device_id_type=MESH
        )

    @pl.when(o > 0)
    def _():
        pl.semaphore_signal(barrier, inc=1, device_id=(o - 1, i, h), device_id_type=MESH)

    @pl.when(o < n_outer - 1)
    def _():
        pl.semaphore_signal(barrier, inc=1, device_id=(o + 1, i, h), device_id_type=MESH)

    behind = jnp.where(o > 0, 1, 0)
    ahead = jnp.where(o < n_outer - 1, 1, 0)
    pl.semaphore_wait(barrier, 1 + n_inner + behind + ahead)

    bufs = (kbuf, vbuf)
    hbms = (k_hbm, v_hbm)

    def z_copy(t, d):
        src = hbms[t] if d == 0 else bufs[t].at[d, i]
        return pltpu.make_async_remote_copy(
            src_ref=src, dst_ref=bufs[t].at[d + 1, i],
            send_sem=z_send.at[t, d], recv_sem=kv_recv.at[t, d + 1, i],
            device_id=(o + 1, i, h), device_id_type=MESH,
        )

    def x_copy(t, d, r):
        src = hbms[t] if d == 0 else bufs[t].at[d, i]
        return pltpu.make_async_remote_copy(
            src_ref=src, dst_ref=bufs[t].at[d, i],
            send_sem=x_send.at[t, d, r], recv_sem=kv_recv.at[t, d, i],
            device_id=(o, lax.rem(i + r, n_inner), h), device_id_type=MESH,
        )

    def arrival(t, d, j):
        return pltpu.make_async_remote_copy(
            src_ref=bufs[t].at[d, j], dst_ref=bufs[t].at[d, j],
            send_sem=z_send.at[t, 0], recv_sem=kv_recv.at[t, d, j],
            device_id=(o, lax.rem(i + 1, n_inner), h), device_id_type=MESH,
        )

    def z_ok(d):
        return (o >= d) & (o < n_outer - 1)

    def forward(t, d):
        if d < reach:
            @pl.when(z_ok(d))
            def _():
                z_copy(t, d).start()
        for r in range(1, n_inner):
            @pl.when(sends_x(d, lax.rem(i + r, n_inner)))
            def _():
                x_copy(t, d, r).start()

    for t in range(2):
        forward(t, 0)
    for w_load in w_loads:
        w_load.start()

    coef = HEAD_SIZE ** (-0.5) * math.log2(math.e)
    start_pos = (o * n_inner + i) * tok

    def visit(d):
        for r in range(1, n_inner):
            j = lax.rem(i + r, n_inner)

            @pl.when(used(d, j))
            def _():
                for t in range(2):
                    arrival(t, d, j).wait_recv()
        k = kbuf[d].reshape(group_len, HEAD_SIZE)
        v_t = vbuf[d].reshape(group_len, HEAD_SIZE).T
        key_pos = (o - d) * group_len + lax.broadcasted_iota(jnp.int32, (group_len, tok), 0)
        query_pos = start_pos + lax.broadcasted_iota(jnp.int32, (group_len, tok), 1)
        starts = ds_v[...].reshape(1, tok)
        visible = (key_pos >= starts) & (key_pos <= query_pos)
        for g in range(heads):
            q = q_v[:, g * HEAD_SIZE:(g + 1) * HEAD_SIZE]
            s = lax.dot_general(k, q, (((1,), (1,)), ((), ())), preferred_element_type=jnp.float32)
            s = jnp.where(visible, s, masked_fill)
            top = jnp.max(s, axis=0, keepdims=True)
            if d == 0:
                peak = top
            else:
                peak = jnp.maximum(m_ref[g:g + 1], top)
                fade = jnp.exp2((m_ref[g:g + 1] - peak) * coef)
            p = jnp.exp2((s - peak) * coef)
            total = jnp.sum(p, axis=0, keepdims=True)
            mixed = jnp.dot(v_t, p.astype(jnp.bfloat16), preferred_element_type=jnp.float32)
            if d > 0:
                total = total + l_ref[g:g + 1] * fade
                mixed = mixed + acc[g] * fade
            if d < reach:
                m_ref[g:g + 1] = peak
                l_ref[g:g + 1] = total
                acc[g] = mixed
            else:
                att[:, g * HEAD_SIZE:(g + 1) * HEAD_SIZE] = (
                    (mixed * (1.0 / total)).T.astype(jnp.bfloat16)
                )

    for load in loads:
        load.wait()
    for d in range(1, reach + 1):
        for t in range(2):
            @pl.when(o >= d)
            def _():
                arrival(t, d, i).wait_recv()
            forward(t, d)
        visit(d - 1)
    visit(reach)

    def to_pair(c):
        return pltpu.make_async_remote_copy(
            src_ref=p_other.at[c], dst_ref=p_recv.at[c],
            send_sem=pair_s.at[c], recv_sem=pair_r.at[c],
            device_id=pair_dev, device_id_type=MESH,
        )

    def to_y(c):
        return pltpu.make_async_remote_copy(
            src_ref=a_own.at[c], dst_ref=y_recv.at[c],
            send_sem=ypush_s.at[c], recv_sem=ypush_r.at[c],
            device_id=y_dev, device_id_type=MESH,
        )

    def sum_to_pair(c):
        return pltpu.make_async_remote_copy(
            src_ref=a_own.at[c], dst_ref=a_recv.at[c],
            send_sem=asum_s.at[c], recv_sem=asum_r.at[c],
            device_id=pair_dev, device_id_type=MESH,
        )

    def relay(c):
        return pltpu.make_async_remote_copy(
            src_ref=y_recv.at[c], dst_ref=y_pair.at[c],
            send_sem=relay_s.at[c], recv_sem=relay_r.at[c],
            device_id=pair_dev, device_id_type=MESH,
        )

    def product(slot):
        w_loads[slot].wait()
        return jnp.dot(att[...], wbuf[slot], preferred_element_type=jnp.float32).astype(jnp.bfloat16)

    def join(c):
        to_pair(c).wait_recv()
        a_own[c] = (
            p_own[c].astype(jnp.float32) + p_recv[c].astype(jnp.float32)
        ).astype(jnp.bfloat16)
        to_y(c).start()
        sum_to_pair(c).start()

    for c in range(n_chunk):
        p_other[c] = product(2 * c)
        to_pair(c).start()
        p_own[c] = product(2 * c + 1)
        if c >= 1:
            join(c - 1)
    join(n_chunk - 1)

    def finish(c):
        sum_to_pair(c).wait_recv()
        relay(c).wait_recv()
        col = pl.multiple_of(other_col + c * CHUNK, CHUNK)
        out_ref[:, pl.ds(col, CHUNK)] = (
            a_recv[c].astype(jnp.float32) + y_pair[c].astype(jnp.float32)
        ).astype(jnp.bfloat16)

    for c in range(n_chunk):
        to_y(c).wait_recv()
        relay(c).start()
        col = pl.multiple_of(own_col + c * CHUNK, CHUNK)
        out_ref[:, pl.ds(col, CHUNK)] = (
            a_own[c].astype(jnp.float32) + y_recv[c].astype(jnp.float32)
        ).astype(jnp.bfloat16)
        if c >= 1:
            finish(c - 1)
    finish(n_chunk - 1)

    for t in range(2):
        for d in range(reach + 1):
            if d < reach:
                @pl.when(z_ok(d))
                def _():
                    z_copy(t, d).wait_send()
            for r in range(1, n_inner):
                @pl.when(sends_x(d, lax.rem(i + r, n_inner)))
                def _():
                    x_copy(t, d, r).wait_send()
    for c in range(n_chunk):
        to_pair(c).wait_send()
        to_y(c).wait_send()
        sum_to_pair(c).wait_send()
        relay(c).wait_send()


def shards(n_outer, n_inner, queries, keys, values, doc_start, w_out):
    tok = queries.shape[0]
    heads = queries.shape[1] // HEAD_SIZE
    dout = w_out.shape[1]
    reach = min(8, n_outer // 2)
    n_chunk = dout // 2 // CHUNK
    bf16, f32 = jnp.bfloat16, jnp.float32
    dma = pltpu.SemaphoreType.DMA
    slots = (reach + 1, n_inner, tok, HEAD_SIZE)
    piece = pltpu.VMEM((n_chunk, tok, CHUNK), bf16)
    any_spec = pl.BlockSpec(memory_space=pltpu.HBM)
    return pl.pallas_call(
        functools.partial(kernel, n_outer, n_inner, reach),
        out_shape=pltpu.VMEM((tok, dout), bf16),
        in_specs=[any_spec] * 5,
        out_specs=pl.BlockSpec(memory_space=pltpu.VMEM),
        scratch_shapes=[
            pltpu.VMEM(queries.shape, bf16),
            pltpu.VMEM((tok,), jnp.int32),
            pltpu.VMEM(slots, bf16),
            pltpu.VMEM(slots, bf16),
            pltpu.VMEM((2 * n_chunk, w_out.shape[0], CHUNK), bf16),
            pltpu.VMEM((heads, tok), f32),
            pltpu.VMEM((heads, tok), f32),
            pltpu.VMEM((heads, HEAD_SIZE, tok), f32),
            pltpu.VMEM((tok, heads * HEAD_SIZE), bf16),
            piece, piece, piece, piece, piece, piece, piece,
            dma((4,)),
            dma((2 * n_chunk,)),
            dma((2, reach + 1, n_inner)),
            dma((2, reach)),
            dma((2, reach + 1, n_inner)),
        ] + [dma((n_chunk,))] * 8,
        compiler_params=pltpu.CompilerParams(
            collective_id=0, has_side_effects=True, vmem_limit_bytes=60 * 1024 * 1024
        ),
    )(queries, keys, values, doc_start, w_out)


def solution(mesh):
    placed = (
        P(("outer", "inner"), "head"),
        P(("outer", "inner"), "head"),
        P(("outer", "inner"), "head"),
        P(("outer", "inner")),
        P("head", None),
    )
    body = functools.partial(shards, mesh.shape["outer"], mesh.shape["inner"])
    return jax.shard_map(
        body, mesh=mesh, in_specs=placed, out_specs=P(("outer", "inner"), None), check_vma=False
    )
```

```python
import functools
import math

import jax
import jax.numpy as jnp
from jax import lax
from jax.experimental import pallas as pl
from jax.experimental.pallas import tpu as pltpu
from jax.sharding import PartitionSpec as P

HEAD_SIZE = 128
CHUNK = 256
PIECES = 1
masked_fill = -1e30
MESH = pl.DeviceIdType.MESH


def kernel(
    n_outer, n_inner, reach,
    q_hbm, k_hbm, v_hbm, ds_hbm, w_hbm, out_ref,
    q_v, ds_v, kbuf, vbuf, wbuf, m_ref, l_ref, acc, att,
    p_other, p_own, p_recv, a_own, a_recv, y_recv, y_pair,
    local_sem, w_sem, kv_recv, z_send, x_send,
    pair_s, pair_r, ypush_s, ypush_r, asum_s, asum_r, relay_s, relay_r,
):
    tok = q_hbm.shape[0]
    heads = q_hbm.shape[1] // HEAD_SIZE
    half = w_hbm.shape[1] // 2
    n_chunk = half // CHUNK
    group_len = tok * n_inner
    o = lax.axis_index("outer")
    i = lax.axis_index("inner")
    h = lax.axis_index("head")
    side = lax.rem(h, 2)
    pair_h = h + 1 - 2 * side
    y_h = lax.rem(h + 2, 4)
    pair_dev = (o, i, pair_h)
    y_dev = (o, i, y_h)

    loads = [
        pltpu.make_async_copy(q_hbm, q_v, local_sem.at[0]),
        pltpu.make_async_copy(ds_hbm, ds_v, local_sem.at[1]),
        pltpu.make_async_copy(k_hbm, kbuf.at[0, i], local_sem.at[2]),
        pltpu.make_async_copy(v_hbm, vbuf.at[0, i], local_sem.at[3]),
    ]
    for load in loads:
        load.start()
    own_col = side * half
    other_col = (1 - side) * half
    w_loads = []
    for c in range(n_chunk):
        for which, base in ((0, other_col), (1, own_col)):
            col = pl.multiple_of(base + c * CHUNK, CHUNK)
            w_loads.append(
                pltpu.make_async_copy(
                    w_hbm.at[:, pl.ds(col, CHUNK)], wbuf.at[2 * c + which], w_sem.at[2 * c + which]
                )
            )

    def used(d, j):
        ok = o >= d
        if d == 0:
            ok = ok & (j <= i)
        if d == reach:
            ok = ok & (j >= i)
        return ok

    def sends_x(d, j):
        ok = o >= d
        if d == 0:
            ok = ok & (j > i)
        if d == reach:
            ok = ok & (j < i)
        return ok

    zeros = jnp.zeros((tok, HEAD_SIZE), jnp.bfloat16)
    for d in range(reach + 1):
        for r in range(n_inner):
            if d == 0 and r == 0:
                continue
            j = lax.rem(i + r, n_inner)

            @pl.when(jnp.logical_not(used(d, j)))
            def _(d=d, j=j):
                kbuf[d, j] = zeros
                vbuf[d, j] = zeros

    barrier = pltpu.get_barrier_semaphore()
    for peer in (pair_dev, y_dev):
        pl.semaphore_signal(barrier, inc=1, device_id=peer, device_id_type=MESH)
    for r in range(1, n_inner):
        pl.semaphore_signal(
            barrier, inc=1, device_id=(o, lax.rem(i + r, n_inner), h), device_id_type=MESH
        )

    @pl.when(o > 0)
    def _():
        pl.semaphore_signal(barrier, inc=1, device_id=(o - 1, i, h), device_id_type=MESH)

    @pl.when(o < n_outer - 1)
    def _():
        pl.semaphore_signal(barrier, inc=1, device_id=(o + 1, i, h), device_id_type=MESH)

    behind = jnp.where(o > 0, 1, 0)
    ahead = jnp.where(o < n_outer - 1, 1, 0)
    for load in loads:
        load.wait()
    pl.semaphore_wait(barrier, 1 + n_inner + behind + ahead)

    bufs = (kbuf, vbuf)

    rows = tok // PIECES

    def part(t, d, j, p):
        return bufs[t].at[d, j, pl.ds(p * rows, rows)]

    def z_copy(t, d, p):
        return pltpu.make_async_remote_copy(
            src_ref=part(t, d, i, p), dst_ref=part(t, d + 1, i, p),
            send_sem=z_send.at[t, d, p], recv_sem=kv_recv.at[t, d + 1, i, p],
            device_id=(o + 1, i, h), device_id_type=MESH,
        )

    def x_copy(t, d, r, p):
        return pltpu.make_async_remote_copy(
            src_ref=part(t, d, i, p), dst_ref=part(t, d, i, p),
            send_sem=x_send.at[t, d, r, p], recv_sem=kv_recv.at[t, d, i, p],
            device_id=(o, lax.rem(i + r, n_inner), h), device_id_type=MESH,
        )

    def arrival(t, d, j, p):
        return pltpu.make_async_remote_copy(
            src_ref=part(t, d, j, p), dst_ref=part(t, d, j, p),
            send_sem=z_send.at[t, 0, p], recv_sem=kv_recv.at[t, d, j, p],
            device_id=(o, lax.rem(i + 1, n_inner), h), device_id_type=MESH,
        )

    def z_ok(d):
        return (o >= d) & (o < n_outer - 1)

    def forward(t, d, p):
        if d < reach:
            @pl.when(z_ok(d))
            def _():
                z_copy(t, d, p).start()
        for r in range(1, n_inner):
            @pl.when(sends_x(d, lax.rem(i + r, n_inner)))
            def _():
                x_copy(t, d, r, p).start()

    for t in range(2):
        for p in range(PIECES):
            forward(t, 0, p)

    coef = HEAD_SIZE ** (-0.5) * math.log2(math.e)
    start_pos = (o * n_inner + i) * tok

    def visit(d):
        for r in range(1, n_inner):
            j = lax.rem(i + r, n_inner)

            @pl.when(used(d, j))
            def _():
                for t in range(2):
                    for p in range(PIECES):
                        arrival(t, d, j, p).wait_recv()
        k = kbuf[d].reshape(group_len, HEAD_SIZE)
        v_t = vbuf[d].reshape(group_len, HEAD_SIZE).T
        key_pos = (o - d) * group_len + lax.broadcasted_iota(jnp.int32, (group_len, tok), 0)
        query_pos = start_pos + lax.broadcasted_iota(jnp.int32, (group_len, tok), 1)
        starts = ds_v[...].reshape(1, tok)
        visible = (key_pos >= starts) & (key_pos <= query_pos)
        for g in range(heads):
            q = q_v[:, g * HEAD_SIZE:(g + 1) * HEAD_SIZE]
            s = lax.dot_general(k, q, (((1,), (1,)), ((), ())), preferred_element_type=jnp.float32)
            s = jnp.where(visible, s, masked_fill)
            top = jnp.max(s, axis=0, keepdims=True)
            if d == 0:
                peak = top
            else:
                peak = jnp.maximum(m_ref[g:g + 1], top)
                fade = jnp.exp2((m_ref[g:g + 1] - peak) * coef)
            p = jnp.exp2((s - peak) * coef)
            total = jnp.sum(p, axis=0, keepdims=True)
            mixed = jnp.dot(v_t, p.astype(jnp.bfloat16), preferred_element_type=jnp.float32)
            if d > 0:
                total = total + l_ref[g:g + 1] * fade
                mixed = mixed + acc[g] * fade
            if d < reach:
                m_ref[g:g + 1] = peak
                l_ref[g:g + 1] = total
                acc[g] = mixed
            else:
                att[:, g * HEAD_SIZE:(g + 1) * HEAD_SIZE] = (
                    (mixed * (1.0 / total)).T.astype(jnp.bfloat16)
                )

    for d in range(1, reach + 1):
        for t in range(2):
            for p in range(PIECES):
                @pl.when(o >= d)
                def _():
                    arrival(t, d, i, p).wait_recv()
                forward(t, d, p)
        if d == 1:
            for w_load in w_loads:
                w_load.start()
        visit(d - 1)
    visit(reach)

    def to_pair(c):
        return pltpu.make_async_remote_copy(
            src_ref=p_other.at[c], dst_ref=p_recv.at[c],
            send_sem=pair_s.at[c], recv_sem=pair_r.at[c],
            device_id=pair_dev, device_id_type=MESH,
        )

    def to_y(c):
        return pltpu.make_async_remote_copy(
            src_ref=a_own.at[c], dst_ref=y_recv.at[c],
            send_sem=ypush_s.at[c], recv_sem=ypush_r.at[c],
            device_id=y_dev, device_id_type=MESH,
        )

    def sum_to_pair(c):
        return pltpu.make_async_remote_copy(
            src_ref=a_own.at[c], dst_ref=a_recv.at[c],
            send_sem=asum_s.at[c], recv_sem=asum_r.at[c],
            device_id=pair_dev, device_id_type=MESH,
        )

    def relay(c):
        return pltpu.make_async_remote_copy(
            src_ref=y_recv.at[c], dst_ref=y_pair.at[c],
            send_sem=relay_s.at[c], recv_sem=relay_r.at[c],
            device_id=pair_dev, device_id_type=MESH,
        )

    def product(slot):
        w_loads[slot].wait()
        return jnp.dot(att[...], wbuf[slot], preferred_element_type=jnp.float32).astype(jnp.bfloat16)

    def join(c):
        to_pair(c).wait_recv()
        a_own[c] = (
            p_own[c].astype(jnp.float32) + p_recv[c].astype(jnp.float32)
        ).astype(jnp.bfloat16)
        to_y(c).start()
        sum_to_pair(c).start()

    for c in range(n_chunk):
        p_other[c] = product(2 * c)
        to_pair(c).start()
        p_own[c] = product(2 * c + 1)
        if c >= 1:
            join(c - 1)
    join(n_chunk - 1)

    def finish(c):
        sum_to_pair(c).wait_recv()
        relay(c).wait_recv()
        col = pl.multiple_of(other_col + c * CHUNK, CHUNK)
        out_ref[:, pl.ds(col, CHUNK)] = (
            a_recv[c].astype(jnp.float32) + y_pair[c].astype(jnp.float32)
        ).astype(jnp.bfloat16)

    for c in range(n_chunk):
        to_y(c).wait_recv()
        relay(c).start()
        col = pl.multiple_of(own_col + c * CHUNK, CHUNK)
        out_ref[:, pl.ds(col, CHUNK)] = (
            a_own[c].astype(jnp.float32) + y_recv[c].astype(jnp.float32)
        ).astype(jnp.bfloat16)
        if c >= 1:
            finish(c - 1)
    finish(n_chunk - 1)

    for t in range(2):
        for d in range(reach + 1):
            for p in range(PIECES):
                if d < reach:
                    @pl.when(z_ok(d))
                    def _():
                        z_copy(t, d, p).wait_send()
                for r in range(1, n_inner):
                    @pl.when(sends_x(d, lax.rem(i + r, n_inner)))
                    def _():
                        x_copy(t, d, r, p).wait_send()
    for c in range(n_chunk):
        to_pair(c).wait_send()
        to_y(c).wait_send()
        sum_to_pair(c).wait_send()
        relay(c).wait_send()


def shards(n_outer, n_inner, queries, keys, values, doc_start, w_out):
    tok = queries.shape[0]
    heads = queries.shape[1] // HEAD_SIZE
    dout = w_out.shape[1]
    reach = min(8, n_outer // 2)
    n_chunk = dout // 2 // CHUNK
    bf16, f32 = jnp.bfloat16, jnp.float32
    dma = pltpu.SemaphoreType.DMA
    slots = (reach + 1, n_inner, tok, HEAD_SIZE)
    piece = pltpu.VMEM((n_chunk, tok, CHUNK), bf16)
    any_spec = pl.BlockSpec(memory_space=pltpu.HBM)
    return pl.pallas_call(
        functools.partial(kernel, n_outer, n_inner, reach),
        out_shape=pltpu.VMEM((tok, dout), bf16),
        in_specs=[any_spec] * 5,
        out_specs=pl.BlockSpec(memory_space=pltpu.VMEM),
        scratch_shapes=[
            pltpu.VMEM(queries.shape, bf16),
            pltpu.VMEM((tok,), jnp.int32),
            pltpu.VMEM(slots, bf16),
            pltpu.VMEM(slots, bf16),
            pltpu.VMEM((2 * n_chunk, w_out.shape[0], CHUNK), bf16),
            pltpu.VMEM((heads, tok), f32),
            pltpu.VMEM((heads, tok), f32),
            pltpu.VMEM((heads, HEAD_SIZE, tok), f32),
            pltpu.VMEM((tok, heads * HEAD_SIZE), bf16),
            piece, piece, piece, piece, piece, piece, piece,
            dma((4,)),
            dma((2 * n_chunk,)),
            dma((2, reach + 1, n_inner, PIECES)),
            dma((2, reach, PIECES)),
            dma((2, reach + 1, n_inner, PIECES)),
        ] + [dma((n_chunk,))] * 8,
        compiler_params=pltpu.CompilerParams(
            collective_id=0, has_side_effects=True, vmem_limit_bytes=60 * 1024 * 1024
        ),
    )(queries, keys, values, doc_start, w_out)


def solution(mesh):
    placed = (
        P(("outer", "inner"), "head"),
        P(("outer", "inner"), "head"),
        P(("outer", "inner"), "head"),
        P(("outer", "inner")),
        P("head", None),
    )
    body = functools.partial(shards, mesh.shape["outer"], mesh.shape["inner"])
    return jax.shard_map(
        body, mesh=mesh, in_specs=placed, out_specs=P(("outer", "inner"), None), check_vma=False
    )
```
